32 devices in a mesh: dp: 32 (over z, y, x, core).
Axes of the slice: x: 2, y: 2, z: 4, core: 2. Of those that a mesh axis runs over, the one named last changes fastest.
Arguments:
- images: float32 [64, 197, 768], P('dp'), may hold values from -6 to 6
- image_count: int32 [32], P('dp'), may hold values from 1 to 2, as said below
- ln1_gain: bfloat16 [2, 768], P(None, 'dp'), may hold values from 0.5 to 1.5
- ln1_bias: bfloat16 [2, 768], P(None, 'dp'), may hold values from -4 to 4
- w_qkv: bfloat16 [2, 768, 2304], P(None, 'dp'), may hold values from -0.21875 to 0.21875
- q_bias: bfloat16 [2, 768], P(None, 'dp'), may hold values from -4 to 4
- v_bias: bfloat16 [2, 768], P(None, 'dp'), may hold values from -4 to 4
- w_out: bfloat16 [2, 768, 768], P(None, 'dp'), may hold values from -0.625 to 0.625
- out_bias: bfloat16 [2, 768], P(None, 'dp'), may hold values from -4 to 4
- ln2_gain: bfloat16 [2, 768], P(None, 'dp'), may hold values from 0.5 to 1.5
- ln2_bias: bfloat16 [2, 768], P(None, 'dp'), may hold values from -4 to 4
- w_up: bfloat16 [2, 768, 3072], P(None, 'dp'), may hold values from -0.21875 to 0.21875
- up_bias: bfloat16 [2, 3072], P(None, 'dp'), may hold values from -4 to 4
- w_down: bfloat16 [2, 3072, 768], P(None, 'dp'), may hold values from -0.109375 to 0.109375
- down_bias: bfloat16 [2, 768], P(None, 'dp'), may hold values from -4 to 4
- cotangent: float32 [64, 197, 768], P('dp'), may hold values from -6 to 6
Outputs:
- output: float32 [64, 197, 768], P('dp')
- input_grad: float32 [64, 197, 768], P('dp')
- grad_ln1_gain: float32 [2, 768], P(None, 'dp')
- grad_ln1_bias: float32 [2, 768], P(None, 'dp')
- grad_w_qkv: float32 [2, 768, 2304], P(None, 'dp')
- grad_q_bias: float32 [2, 768], P(None, 'dp')
- grad_v_bias: float32 [2, 768], P(None, 'dp')
- grad_w_out: float32 [2, 768, 768], P(None, 'dp')
- grad_out_bias: float32 [2, 768], P(None, 'dp')
- grad_ln2_gain: float32 [2, 768], P(None, 'dp')
- grad_ln2_bias: float32 [2, 768], P(None, 'dp')
- grad_w_up: float32 [2, 768, 3072], P(None, 'dp')
- grad_up_bias: float32 [2, 3072], P(None, 'dp')
- grad_w_down: float32 [2, 3072, 768], P(None, 'dp')
- grad_down_bias: float32 [2, 768], P(None, 'dp')
The draws below stay inside these ranges and needn't reach their ends.
Inputs may be any that keep to these rules, and one draw needn't show every extreme that they name: `image_count`: every device holds 1 or 2 images; exactly 20 devices hold 2.
All inputs are finite; a program needn't handle non-finite values.
Results may differ from the reference program's by a relative error of at most 0.01.
Values may be sent and summed in bfloat16 or wider, within the bound.
No kernel may reach another device: no remote copies, remote signals or barrier semaphores. Data moves between devices by JAX's collectives and lax.ppermute only.
A program may use at most 448 MiB of HBM per device.

```python
import jax
import jax.numpy as jnp
from jax import lax

D = 768
HEADS = 12
FF = 3072
S = 197
L = 2
SLOTS = 2
EXTRA = 20
IMAGES = 52
TOTAL_SLOTS = 64
N_DP = 32


def draw_image_count(key, part):
    order = jax.random.permutation(key, N_DP)
    return (1 + (order < EXTRA).astype(jnp.int32)).astype(jnp.int32)


def level_of(key, shape, shards, low, top_value):
    def one(axis_at, parts):
        heights = jax.random.uniform(jax.random.fold_in(jax.random.fold_in(key, 6), axis_at), (parts,), jnp.float32, low / len(shards), top_value / len(shards))
        return jnp.repeat(jnp.exp(heights), shape[axis_at] // parts).reshape((-1,) + (1,) * (len(shape) - axis_at - 1))

    factor_of = one(*shards[0])
    for cut in shards[1:]:
        factor_of = factor_of * one(*cut)
    return factor_of


def gaussian(own_key, extent, deviation, reach, split=(), kind=jnp.bfloat16):
    values = deviation * jax.random.normal(own_key, extent, jnp.float32)
    if split:
        values = values * level_of(own_key, extent, split, -0.22, 0.18)
    return jnp.clip(values, -reach, reach).astype(kind)


def setup_inputs(seed: int = 0) -> dict:
    keys = jax.random.split(jax.random.key(seed), 17)
    images = gaussian(keys[0], (TOTAL_SLOTS, S, D), 1.0, 6.0, ((0, 32),), jnp.float32)
    image_count = draw_image_count(jax.random.fold_in(keys[16], 71), 0)
    ln1_gain = jnp.clip(1.0 + 0.1 * jax.random.normal(keys[2], (L, D), jnp.float32), 0.5, 1.5).astype(jnp.bfloat16)
    ln1_bias = gaussian(keys[3], (L, D), 0.3, 4.0, ((1, 32),))
    w_qkv = gaussian(keys[4], (L, D, 3 * D), D ** -0.5, 0.21875, ((1, 32),))
    q_bias = gaussian(keys[5], (L, D), 0.3, 4.0, ((1, 32),))
    v_bias = gaussian(keys[6], (L, D), 0.3, 4.0, ((1, 32),))
    w_out = gaussian(keys[7], (L, D, D), (D // 8) ** -0.5, 0.625, ((1, 32),))
    out_bias = gaussian(keys[8], (L, D), 0.3, 4.0, ((1, 32),))
    ln2_gain = jnp.clip(1.0 + 0.1 * jax.random.normal(keys[9], (L, D), jnp.float32), 0.5, 1.5).astype(jnp.bfloat16)
    ln2_bias = gaussian(keys[10], (L, D), 0.3, 4.0, ((1, 32),))
    w_up = gaussian(keys[11], (L, D, FF), D ** -0.5, 0.21875, ((1, 32),))
    up_bias = gaussian(keys[12], (L, FF), 0.3, 4.0, ((1, 32),))
    w_down = gaussian(keys[13], (L, FF, D), FF ** -0.5, 0.109375, ((1, 32),))
    down_bias = gaussian(keys[14], (L, D), 0.3, 4.0, ((1, 32),))
    cotangent = gaussian(keys[15], (TOTAL_SLOTS, S, D), 1.0, 6.0, ((0, 32),), jnp.float32)
    return dict(images=images, image_count=image_count, ln1_gain=ln1_gain, ln1_bias=ln1_bias, w_qkv=w_qkv, q_bias=q_bias, v_bias=v_bias, w_out=w_out, out_bias=out_bias, ln2_gain=ln2_gain, ln2_bias=ln2_bias, w_up=w_up, up_bias=up_bias, w_down=w_down, down_bias=down_bias, cotangent=cotangent)


EPS = 1e-06
SCALE = 0.125

def product(form, left, right):
    return jnp.einsum(form, left.astype(jnp.float32), right.astype(jnp.float32))

def norm_forward(stream, gain_vec, shift_vec):
    center = stream - lax.optimization_barrier(jnp.mean(stream, axis=-1, keepdims=True))
    inverse = lax.rsqrt(lax.optimization_barrier(jnp.mean(center * center, axis=-1, keepdims=True)) + EPS)
    normed = center * inverse
    return (normed * gain_vec.astype(jnp.float32) + shift_vec.astype(jnp.float32), normed, inverse)

def norm_backward(upstream, normed, inverse, gain_vec):
    scaled = upstream * gain_vec.astype(jnp.float32)
    return inverse * (scaled - lax.optimization_barrier(jnp.mean(scaled, axis=-1, keepdims=True)) - normed * lax.optimization_barrier(jnp.mean(scaled * normed, axis=-1, keepdims=True)))

def gelu_tanh(argument):
    return jax.nn.gelu(argument, approximate=True)

def layer_forward(stream, weights):
    gain_one, shift_one, w_mixed, query_bias, value_bias, w_proj, proj_bias, gain_two, shift_two, w_first, first_bias, w_second, second_bias = weights
    seq_len = stream.shape[0]
    model_width = stream.shape[1]
    head_size = model_width // HEADS
    normed_in, norm_one, inv_one = norm_forward(stream, gain_one, shift_one)
    entered = normed_in.astype(jnp.bfloat16)
    qkv_mixed = jnp.dot(entered, w_mixed, preferred_element_type=jnp.float32)
    query_heads = (qkv_mixed[:, :model_width] + query_bias.astype(jnp.float32)).astype(jnp.bfloat16).reshape(seq_len, HEADS, head_size)
    key_heads = qkv_mixed[:, model_width:2 * model_width].astype(jnp.bfloat16).reshape(seq_len, HEADS, head_size)
    value_heads = (qkv_mixed[:, 2 * model_width:] + value_bias.astype(jnp.float32)).astype(jnp.bfloat16).reshape(seq_len, HEADS, head_size)
    scores = product('qhd,khd->hqk', query_heads, key_heads) * SCALE
    row_max = lax.optimization_barrier(jnp.max(scores, axis=-1, keepdims=True))
    shifted = jnp.exp(scores - row_max)
    soft_probs = shifted / lax.optimization_barrier(jnp.sum(shifted, axis=-1, keepdims=True))
    probs_low = soft_probs.astype(jnp.bfloat16)
    attended = product('hqk,khd->qhd', probs_low, value_heads).reshape(seq_len, model_width).astype(jnp.bfloat16)
    middle = stream + jnp.dot(attended, w_proj, preferred_element_type=jnp.float32) + proj_bias.astype(jnp.float32)
    normed_mid, norm_two, inv_two = norm_forward(middle, gain_two, shift_two)
    hidden_in = normed_mid.astype(jnp.bfloat16)
    pre_act = jnp.dot(hidden_in, w_first, preferred_element_type=jnp.float32) + first_bias.astype(jnp.float32)
    activated = gelu_tanh(pre_act).astype(jnp.bfloat16)
    result = middle + jnp.dot(activated, w_second, preferred_element_type=jnp.float32) + second_bias.astype(jnp.float32)
    cached = (norm_one, inv_one, entered, query_heads, key_heads, value_heads, soft_probs, probs_low, attended, norm_two, inv_two, hidden_in, pre_act, activated)
    return (result, cached)

def layer_backward(stream, weights, upstream):
    gain_one, shift_one, w_mixed, query_bias, value_bias, w_proj, proj_bias, gain_two, shift_two, w_first, first_bias, w_second, second_bias = weights
    unused, cached = layer_forward(stream, weights)
    norm_one, inv_one, entered, query_heads, key_heads, value_heads, soft_probs, probs_low, attended, norm_two, inv_two, hidden_in, pre_act, activated = cached
    seq_len = stream.shape[0]
    model_width = stream.shape[1]
    head_size = model_width // HEADS
    up_low = upstream.astype(jnp.bfloat16)
    grad_second = jnp.dot(activated.T, up_low, preferred_element_type=jnp.float32)
    grad_second_bias = lax.optimization_barrier(jnp.sum(upstream, axis=0))
    grad_act = jnp.dot(up_low, w_second.T, preferred_element_type=jnp.float32)
    grad_pre = jax.vjp(gelu_tanh, pre_act)[1](grad_act)[0]
    pre_low = grad_pre.astype(jnp.bfloat16)
    grad_first = jnp.dot(hidden_in.T, pre_low, preferred_element_type=jnp.float32)
    grad_first_bias = lax.optimization_barrier(jnp.sum(grad_pre, axis=0))
    grad_hidden = jnp.dot(pre_low, w_first.T, preferred_element_type=jnp.float32)
    grad_gain_two = lax.optimization_barrier(jnp.sum(grad_hidden * norm_two, axis=0))
    grad_shift_two = lax.optimization_barrier(jnp.sum(grad_hidden, axis=0))
    grad_middle = upstream + norm_backward(grad_hidden, norm_two, inv_two, gain_two)
    mid_low = grad_middle.astype(jnp.bfloat16)
    grad_proj = jnp.dot(attended.T, mid_low, preferred_element_type=jnp.float32)
    grad_proj_bias = lax.optimization_barrier(jnp.sum(grad_middle, axis=0))
    grad_att = jnp.dot(mid_low, w_proj.T, preferred_element_type=jnp.float32).astype(jnp.bfloat16).reshape(seq_len, HEADS, head_size)
    grad_probs = product('qhd,khd->hqk', grad_att, value_heads)
    grad_values = product('hqk,qhd->khd', probs_low, grad_att).reshape(seq_len, model_width)
    row_inner = lax.optimization_barrier(jnp.sum(soft_probs * grad_probs, axis=-1, keepdims=True))
    grad_scores = (soft_probs * (grad_probs - row_inner) * SCALE).astype(jnp.bfloat16)
    grad_query = product('hqk,khd->qhd', grad_scores, key_heads).reshape(seq_len, model_width)
    grad_keys = product('hqk,qhd->khd', grad_scores, query_heads).reshape(seq_len, model_width)
    grad_query_bias = lax.optimization_barrier(jnp.sum(grad_query, axis=0))
    grad_value_bias = lax.optimization_barrier(jnp.sum(grad_values, axis=0))
    grad_joined = jnp.concatenate([grad_query, grad_keys, grad_values], axis=1).astype(jnp.bfloat16)
    grad_mixed = jnp.dot(entered.T, grad_joined, preferred_element_type=jnp.float32)
    grad_entered = jnp.dot(grad_joined, w_mixed.T, preferred_element_type=jnp.float32)
    grad_gain_one = lax.optimization_barrier(jnp.sum(grad_entered * norm_one, axis=0))
    grad_shift_one = lax.optimization_barrier(jnp.sum(grad_entered, axis=0))
    grad_stream = grad_middle + norm_backward(grad_entered, norm_one, inv_one, gain_one)
    return (grad_stream, (grad_gain_one, grad_shift_one, grad_mixed, grad_query_bias, grad_value_bias, grad_proj, grad_proj_bias, grad_gain_two, grad_shift_two, grad_first, grad_first_bias, grad_second, grad_second_bias))

def reference(images, image_count, ln1_gain, ln1_bias, w_qkv, q_bias, v_bias, w_out, out_bias, ln2_gain, ln2_bias, w_up, up_bias, w_down, down_bias, cotangent):
    params = (ln1_gain, ln1_bias, w_qkv, q_bias, v_bias, w_out, out_bias, ln2_gain, ln2_bias, w_up, up_bias, w_down, down_bias)
    layer_total = ln1_gain.shape[0]
    position = jnp.arange(images.shape[0], dtype=jnp.int32)
    owner_count = jnp.repeat(image_count.astype(jnp.int32), SLOTS)
    is_live = position % SLOTS < owner_count
    chosen = jnp.nonzero(is_live, size=IMAGES)[0].astype(jnp.int32)

    def visit_image(totals, slot_index):
        stream = images[slot_index]
        upstream = cotangent[slot_index]
        inputs = []
        for layer_index in range(layer_total):
            inputs.append(stream)
            stream, unused = layer_forward(stream, tuple((tensor[layer_index] for tensor in params)))
        result = stream
        per_layer = [None] * layer_total
        for layer_index in reversed(range(layer_total)):
            upstream, grad_list = layer_backward(inputs[layer_index], tuple((tensor[layer_index] for tensor in params)), upstream)
            per_layer[layer_index] = grad_list
        totals = tuple((total + jnp.stack([per_layer[layer_index][member] for layer_index in range(layer_total)]) for member, total in enumerate(totals)))
        return (totals, (result, upstream))
    initial = tuple((jnp.zeros(tensor.shape, jnp.float32) for tensor in params))
    totals, (results, grads_in) = lax.scan(visit_image, initial, chosen)
    output = jnp.zeros(images.shape, jnp.float32).at[chosen].set(results)
    input_grad = jnp.zeros(images.shape, jnp.float32).at[chosen].set(grads_in)
    return (output, input_grad, totals[0], totals[1], totals[2], totals[3], totals[4], totals[5], totals[6], totals[7], totals[8], totals[9], totals[10], totals[11], totals[12])
```

```python
import functools

import jax
import jax.numpy as jnp
from jax import lax
from jax.experimental import pallas as pl
from jax.experimental.pallas import tpu as pltpu
from jax.sharding import PartitionSpec as P

HEADS = 12
EPS = 1e-06
SCALE = 0.125
CUBE = 32
BF = jnp.bfloat16
F32 = jnp.float32


def flip(value, bits):
    return lax.ppermute(value, "dp", [(i, i ^ bits) for i in range(CUBE)])


def add_low(one, two):
    return (one.astype(F32) + two.astype(F32)).astype(BF)


def place_kernel(*refs):
    pieces, whole, sem = refs[:8], refs[8], refs[9]
    me = lax.axis_index("dp")
    copies = [
        pltpu.make_async_copy(pieces[k].at[z], whole.at[me ^ (z * 8 + k)], sem.at[z * 8 + k])
        for k in range(8)
        for z in range(4)
    ]
    for copy in copies:
        copy.start()
    for copy in copies:
        copy.wait()


def place(pieces):
    z, rows, cols = pieces[0].shape
    out = pl.pallas_call(
        place_kernel,
        out_shape=jax.ShapeDtypeStruct((CUBE, rows, cols), pieces[0].dtype),
        in_specs=[pl.BlockSpec(memory_space=pl.ANY)] * 8,
        out_specs=pl.BlockSpec(memory_space=pltpu.VMEM),
        scratch_shapes=[pltpu.SemaphoreType.DMA((CUBE,))],
        name="place",
    )(*pieces)
    return out.reshape(CUBE * rows, cols)


def split_kernel(*refs):
    whole, pieces, sem = refs[0], refs[1:9], refs[9]
    me = lax.axis_index("dp")
    copies = [
        pltpu.make_async_copy(whole.at[me ^ (z * 8 + k)], pieces[k].at[z], sem.at[z * 8 + k])
        for k in range(8)
        for z in range(4)
    ]
    for copy in copies:
        copy.start()
    for copy in copies:
        copy.wait()


def split(whole):
    rows, cols = whole.shape[0] // CUBE, whole.shape[1]
    return pl.pallas_call(
        split_kernel,
        out_shape=[jax.ShapeDtypeStruct((4, rows, cols), whole.dtype)] * 8,
        in_specs=[pl.BlockSpec(memory_space=pltpu.VMEM)],
        out_specs=[pl.BlockSpec(memory_space=pl.ANY)] * 8,
        scratch_shapes=[pltpu.SemaphoreType.DMA((CUBE,))],
        name="split",
    )(whole.reshape(CUBE, rows, cols))


def gather(shard, order):
    near = jnp.stack([shard, flip(shard, 8), flip(shard, 16), flip(shard, 24)])
    first, second = order
    have = {0: near, first: flip(near, first), second: flip(near, second)}
    have[first | second] = flip(have[first], second)
    for key in (0, first, second, first | second):
        have[key | 1] = flip(have[key], 1)
    return place([have[k] for k in range(8)])


def scatter(whole, order):
    part = split(whole)
    first, second = order
    part = {k: add_low(part[k], flip(part[k | 1], 1)) for k in (first | second, first, second, 0)}
    far = add_low(part[second], flip(part[first | second], first))
    near = add_low(part[0], flip(part[first], first))
    near = add_low(near, flip(far, second))
    total = near[0].astype(F32)
    for z in (1, 2, 3):
        total = total + flip(near[z], 8 * z).astype(F32)
    return total


def gather_small(shard):
    have = jnp.stack([shard, flip(shard, 8), flip(shard, 16), flip(shard, 24)])
    have = jnp.stack([have, flip(have, 4)], axis=1)
    have = jnp.stack([have, flip(have, 2)], axis=2)
    have = jnp.stack([have, flip(have, 1)], axis=3)
    have = have.reshape(CUBE, -1)
    return have[jnp.arange(CUBE) ^ lax.axis_index("dp")]


def scatter_small(rows):
    rows = rows[jnp.arange(CUBE) ^ lax.axis_index("dp")].reshape(4, 2, 2, 2, -1)
    rows = rows[:, :, :, 0] + flip(rows[:, :, :, 1], 1)
    rows = rows[:, :, 0] + flip(rows[:, :, 1], 2)
    rows = rows[:, 0] + flip(rows[:, 1], 4)
    return rows[0] + flip(rows[1], 8) + flip(rows[2], 16) + flip(rows[3], 24)


def weigh(query, key, live):
    scores = lax.dot_general(query, key, (((1,), (1,)), ((), ())), preferred_element_type=F32) * SCALE
    scores = jnp.where(live, scores, -1e30)
    shifted = jnp.exp(scores - jnp.max(scores, axis=-1, keepdims=True))
    return shifted / jnp.sum(shifted, axis=-1, keepdims=True)


def attend_kernel(seq, head, q_ref, k_ref, v_ref, o_ref):
    query, key, value = q_ref[0], k_ref[0], v_ref[0]
    padded, width = query.shape
    live = lax.broadcasted_iota(jnp.int32, (padded, padded), 1) < seq
    lane = lax.broadcasted_iota(jnp.int32, (padded, width), 1) // head
    out = jnp.zeros((padded, width), F32)
    for h in range(width // head):
        mine = lane == h
        probs = weigh(jnp.where(mine, query, jnp.zeros_like(query)), key, live).astype(BF)
        out = jnp.where(mine, jnp.dot(probs, value, preferred_element_type=F32), out)
    o_ref[0] = out.astype(BF)


def attend_back_kernel(seq, head, q_ref, k_ref, v_ref, g_ref, dq_ref, dk_ref, dv_ref, sq_ref, sv_ref):
    query, key, value, grad = q_ref[0], k_ref[0], v_ref[0], g_ref[0]
    padded, width = query.shape
    live = lax.broadcasted_iota(jnp.int32, (padded, padded), 1) < seq
    lane = lax.broadcasted_iota(jnp.int32, (padded, width), 1) // head
    zero = jnp.zeros((padded, width), F32)
    dq, dk, dv = zero, zero, zero
    for h in range(width // head):
        mine = lane == h
        probs = weigh(jnp.where(mine, query, jnp.zeros_like(query)), key, live)
        low = probs.astype(BF)
        grad_h = jnp.where(mine, grad, jnp.zeros_like(grad))
        dp = lax.dot_general(grad_h, value, (((1,), (1,)), ((), ())), preferred_element_type=F32)
        dv = jnp.where(
            mine, lax.dot_general(low, grad, (((0,), (0,)), ((), ())), preferred_element_type=F32), dv
        )
        inner = jnp.sum(probs * dp, axis=-1, keepdims=True)
        ds = (probs * (dp - inner) * SCALE).astype(BF)
        dq = jnp.where(mine, jnp.dot(ds, key, preferred_element_type=F32), dq)
        dk = jnp.where(
            mine, lax.dot_general(ds, query, (((0,), (0,)), ((), ())), preferred_element_type=F32), dk
        )
    dq_ref[0] = dq.astype(BF)
    dk_ref[0] = dk.astype(BF)
    dv_ref[0] = dv.astype(BF)
    sq_ref[0] = jnp.sum(dq, axis=0, keepdims=True)
    sv_ref[0] = jnp.sum(dv, axis=0, keepdims=True)


def lanes(padded, offset, pairs):
    return pl.BlockSpec((1, padded, 128), lambda i, p: (i, 0, offset * pairs + p))


def attend(qkv, seq):
    slots, padded, three = qkv.shape
    width = three // 3
    pairs = width // 128
    return pl.pallas_call(
        functools.partial(attend_kernel, seq, width // HEADS),
        out_shape=jax.ShapeDtypeStruct((slots, padded, width), BF),
        grid=(slots, pairs),
        in_specs=[lanes(padded, part, pairs) for part in range(3)],
        out_specs=lanes(padded, 0, pairs),
        name="attend",
    )(qkv, qkv, qkv)


def attend_back(qkv, grad, seq):
    slots, padded, three = qkv.shape
    width = three // 3
    pairs = width // 128
    side = pl.BlockSpec((1, 1, 128), lambda i, p: (i, 0, p))
    whole = jax.ShapeDtypeStruct((slots, padded, width), BF)
    sums = jax.ShapeDtypeStruct((slots, 1, width), F32)
    return pl.pallas_call(
        functools.partial(attend_back_kernel, seq, width // HEADS),
        out_shape=[whole] * 3 + [sums] * 2,
        grid=(slots, pairs),
        in_specs=[lanes(padded, part, pairs) for part in range(3)] + [lanes(padded, 0, pairs)],
        out_specs=[lanes(padded, 0, pairs)] * 3 + [side] * 2,
        name="attend_back",
    )(qkv, qkv, qkv, grad)


def dot(left, right):
    return jnp.dot(left, right, preferred_element_type=F32)


def outer(left, right):
    return lax.dot_general(left, right, (((0,), (0,)), ((), ())), preferred_element_type=F32)


def times_t(left, right):
    return lax.dot_general(left, right, (((1,), (1,)), ((), ())), preferred_element_type=F32)


def normalize(stream):
    center = stream - jnp.mean(stream, axis=-1, keepdims=True)
    inverse = lax.rsqrt(jnp.mean(center * center, axis=-1, keepdims=True) + EPS)
    return center * inverse, inverse


def norm_backward(upstream, normed, inverse, gain):
    scaled = upstream * gain
    return inverse * (
        scaled
        - jnp.mean(scaled, axis=-1, keepdims=True)
        - normed * jnp.mean(scaled * normed, axis=-1, keepdims=True)
    )


def gelu_tanh(argument):
    return jax.nn.gelu(argument, approximate=True)


def body(
    images,
    image_count,
    ln1_gain,
    ln1_bias,
    w_qkv,
    q_bias,
    v_bias,
    w_out,
    out_bias,
    ln2_gain,
    ln2_bias,
    w_up,
    up_bias,
    w_down,
    down_bias,
    cotangent,
):
    devices = lax.axis_size("dp")
    cube = devices == CUBE
    slots, seq, width = images.shape
    layers = ln1_gain.shape[0]
    padded = -(-seq // 16) * 16
    rows = slots * padded

    vectors = (ln1_gain, ln1_bias, q_bias, v_bias, out_bias, ln2_gain, ln2_bias, down_bias, up_bias)
    sizes = [v.shape[1] for v in vectors]
    packed = jnp.concatenate(vectors, axis=1)
    across = packed.shape[1]
    if cube:
        small = gather_small(packed.reshape(-1)).reshape(devices, layers, across)
    else:
        small = lax.all_gather(packed, "dp")
    small = small.astype(F32)
    named = []
    for layer in range(layers):
        found, at = [], 0
        for size in sizes:
            found.append(small[:, layer, at : at + size].reshape(-1))
            at += size
        named.append(found)

    orders = ((2, 4), (4, 2))
    weights = []
    turn = 0
    for layer in range(layers):
        shards = (
            jnp.concatenate([w_qkv[layer], w_out[layer]], axis=1),
            w_up[layer],
            w_down[layer],
        )
        whole = []
        for shard in shards:
            if cube:
                whole.append(gather(shard, orders[turn % 2]))
            else:
                whole.append(lax.all_gather(shard, "dp", axis=0, tiled=True))
            turn += 1
        weights.append((whole[0][:, : 3 * width], whole[0][:, 3 * width :], whole[1], whole[2]))

    live = lax.broadcasted_iota(jnp.int32, (slots, 1, 1), 0) < image_count[0]

    def enter(tensor):
        tensor = jnp.where(live, tensor, 0.0)
        return jnp.pad(tensor, ((0, 0), (0, padded - seq), (0, 0))).reshape(rows, width)

    stream = enter(images)
    upstream = enter(cotangent)

    saved = []
    for layer in range(layers):
        wq, wo, wu, wd = weights[layer]
        g1, b1, qb, vb, ob, g2, b2, db, ub = named[layer]
        normed, _ = normalize(stream)
        entered = (normed * g1 + b1).astype(BF)
        qkv = (dot(entered, wq) + jnp.concatenate([qb, jnp.zeros_like(qb), vb])).astype(BF)
        mixed = attend(qkv.reshape(slots, padded, 3 * width), seq).reshape(rows, width)
        middle = stream + dot(mixed, wo) + ob
        normed, _ = normalize(middle)
        hidden = (normed * g2 + b2).astype(BF)
        pre = dot(hidden, wu) + ub
        active = gelu_tanh(pre).astype(BF)
        result = middle + dot(active, wd) + db
        saved.append((stream, entered, qkv, mixed, middle, hidden, pre, active))
        stream = result

    output = jnp.where(live, stream.reshape(slots, padded, width)[:, :seq], 0.0)

    def send(grad, turn):
        if cube:
            return scatter(grad, orders[turn % 2])
        return lax.psum_scatter(grad, "dp", scatter_dimension=0, tiled=True).astype(F32)

    big = [None] * layers
    little = [None] * layers
    turn = 0
    for layer in reversed(range(layers)):
        wq, wo, wu, wd = weights[layer]
        g1, b1, qb, vb, ob, g2, b2, db, ub = named[layer]
        stream, entered, qkv, mixed, middle, hidden, pre, active = saved[layer]
        low = upstream.astype(BF)
        s_down = send(outer(active, low).astype(BF), turn)
        sum_down = jnp.sum(upstream, axis=0)
        grad_pre = jax.vjp(gelu_tanh, pre)[1](times_t(low, wd))[0]
        sum_up = jnp.sum(grad_pre, axis=0)
        low = grad_pre.astype(BF)
        s_up = send(outer(hidden, low).astype(BF), turn + 1)
        grad_hidden = times_t(low, wu)
        normed, inverse = normalize(middle)
        sum_g2 = jnp.sum(grad_hidden * normed, axis=0)
        sum_b2 = jnp.sum(grad_hidden, axis=0)
        grad_middle = upstream + norm_backward(grad_hidden, normed, inverse, g2)
        low = grad_middle.astype(BF)
        s_out = send(outer(mixed, low).astype(BF), turn + 1)
        sum_out = jnp.sum(grad_middle, axis=0)
        grad_mixed = times_t(low, wo).astype(BF)
        dq, dk, dv, sum_q, sum_v = attend_back(
            qkv.reshape(slots, padded, 3 * width), grad_mixed.reshape(slots, padded, width), seq
        )
        joined = jnp.concatenate([dq, dk, dv], axis=2).reshape(rows, 3 * width)
        s_qkv = send(outer(entered, joined).astype(BF), turn)
        grad_entered = times_t(joined, wq)
        normed, inverse = normalize(stream)
        sum_g1 = jnp.sum(grad_entered * normed, axis=0)
        sum_b1 = jnp.sum(grad_entered, axis=0)
        upstream = grad_middle + norm_backward(grad_entered, normed, inverse, g1)
        turn += 1
        big[layer] = (s_qkv, s_out, s_up, s_down)
        sums = (sum_g1, sum_b1, sum_q.sum((0, 1)), sum_v.sum((0, 1)), sum_out, sum_g2, sum_b2, sum_down, sum_up)
        little[layer] = jnp.concatenate([s.reshape(devices, -1) for s in sums], axis=1)

    together = jnp.concatenate(little, axis=1)
    if cube:
        own = scatter_small(together)
    else:
        own = lax.psum_scatter(together, "dp", scatter_dimension=0, tiled=True)
    own = own.reshape(layers, across)
    pieces, at = [], 0
    for size in sizes:
        pieces.append(own[:, at : at + size])
        at += size
    p_g1, p_b1, p_q, p_v, p_out, p_g2, p_b2, p_down, p_up = pieces
    s_qkv, s_out, s_up, s_down = (jnp.stack([big[layer][m] for layer in range(layers)]) for m in range(4))
    input_grad = jnp.where(live, upstream.reshape(slots, padded, width)[:, :seq], 0.0)
    return (
        output,
        input_grad,
        p_g1,
        p_b1,
        s_qkv,
        p_q,
        p_v,
        s_out,
        p_out,
        p_g2,
        p_b2,
        s_up,
        p_up,
        s_down,
        p_down,
    )


def solution(mesh):
    rows = P("dp", None, None)
    vector = P(None, "dp")
    matrix = P(None, "dp", None)
    in_specs = (
        rows,
        P("dp"),
        vector,
        vector,
        matrix,
        vector,
        vector,
        matrix,
        vector,
        vector,
        vector,
        matrix,
        vector,
        matrix,
        vector,
        rows,
    )
    out_specs = (
        rows,
        rows,
        vector,
        vector,
        matrix,
        vector,
        vector,
        matrix,
        vector,
        vector,
        vector,
        matrix,
        vector,
        matrix,
        vector,
    )
    return jax.shard_map(body, mesh=mesh, in_specs=in_specs, out_specs=out_specs, check_vma=False)
```
